768 devices in a mesh: dp: 96 (over y, z_lo, core), tensor: 8 (over x, z_hi).
Axes of the slice: x: 4, y: 8, z: 12 (z_hi: 2, z_lo: 6; z = z_hi * 6 + z_lo), core: 2. Of those that a mesh axis runs over, the one named last changes fastest.
Arguments:
- tokens: bfloat16 [12288, 4096], P(('dp', 'tensor')), parts along dimension 0, may hold values from -6 to 6
- gate_act: bfloat16 [12288, 10240], P('dp', 'tensor'), parts along dimension 0, may hold values from -6 to 6
- up_act: bfloat16 [12288, 10240], P('dp', 'tensor'), parts along dimension 0, may hold values from -6 to 6
- down_weight: bfloat16 [10240, 4096], P('tensor'), may hold values from -0.0625 to 0.0625
- norm_gain: float32 [4096], replicated, may hold values from 0.25 to 1.75
Outputs:
- residual_out: bfloat16 [12288, 4096], P(('dp', 'tensor')), parts along dimension 0
- next_rows: bfloat16 [12288, 4096], P('dp'), parts along dimension 0
- next_scale: float32 [12288], P('dp'), parts along dimension 0
The draws below stay inside these ranges and needn't reach their ends.
There are 96 independent parts, one for each index of `dp`. The reference program is written for one: setup_inputs(seed, part) draws one part's arguments, and reference() takes and returns one part's arrays. A program takes and returns all parts, laid end to end along the dimension named above; an argument that names none is the same for every part. Nothing has to cross between parts.
All inputs are finite; a program needn't handle non-finite values. Where the reference program divides by a largest or mean magnitude, that divisor is 1e-20 or more.
Results may differ from the reference program's by a relative error of at most 0.009.
Values may be sent and summed in bfloat16 or wider, within the bound.
A program may use at most 32 MiB of HBM per device.

```python
import jax
import jax.numpy as jnp
from jax import lax

D = 4096
FF_DEV = 1280
TOKENS = 128
FF = 10240
N_TENSOR = 8


def level_of(stream_key, extent, shards, low, largest):
    factor_of, own = 1.0, jax.random.fold_in(stream_key, 6)
    for position, shards_of in shards:
        heights = jnp.exp(jax.random.uniform(jax.random.fold_in(own, position), (shards_of,), jnp.float32, low / len(shards), largest / len(shards)))
        factor_of = factor_of * jnp.repeat(heights, extent[position] // shards_of).reshape([-1 if axis == position else 1 for axis in range(len(extent))])
    return factor_of


def gaussian(own_key, extent, scale, limit, cuts=(), dtype=jnp.bfloat16):
    entries = scale * jax.random.normal(own_key, extent, jnp.float32)
    if cuts:
        entries = entries * level_of(own_key, extent, cuts, -0.22, 0.18)
    return jnp.clip(entries, -limit, limit).astype(dtype)


def setup_inputs(seed: int = 0, part: int = 0) -> dict:
    keys = jax.random.split(jax.random.key(seed), 6)
    part_keys = jax.random.split(jax.random.fold_in(keys[5], part), 6)
    return {
        "tokens": gaussian(part_keys[0], (TOKENS, D), 1.0, 6.0, ((0, 8),)),
        "gate_act": gaussian(part_keys[1], (TOKENS, FF), 1.0, 6.0, ((1, 8),)),
        "up_act": gaussian(part_keys[2], (TOKENS, FF), 1.0, 6.0, ((1, 8),)),
        "down_weight": gaussian(keys[3], (FF, D), FF ** -0.5, 0.0625, ((0, 8),)),
        "norm_gain": jnp.clip(1.0 + 0.15 * jax.random.normal(keys[4], (D,), jnp.float32), 0.25, 1.75),
    }


def reference(tokens, gate_act, up_act, down_weight, norm_gain):
    hidden = (jax.nn.silu(gate_act.astype(jnp.float32)) * up_act.astype(jnp.float32)).astype(jnp.bfloat16)
    total = jnp.zeros((tokens.shape[0], tokens.shape[1]), jnp.float32)
    for group in range(N_TENSOR):
        part_hidden = hidden[:, group * FF_DEV:(group + 1) * FF_DEV]
        part_down = down_weight[group * FF_DEV:(group + 1) * FF_DEV, :]
        product = jnp.dot(part_hidden, part_down, preferred_element_type=jnp.float32)
        rounded = lax.optimization_barrier(product.astype(jnp.bfloat16))
        total = total + rounded.astype(jnp.float32)
    residual = tokens.astype(jnp.float32) + total
    mean_square = lax.optimization_barrier(jnp.mean(residual * residual, axis=1, keepdims=True))
    normed = residual * lax.rsqrt(mean_square + 1e-05) * norm_gain[None, :]
    next_scale = lax.optimization_barrier(jnp.max(jnp.abs(normed), axis=1))
    next_rows = (normed / next_scale[:, None]).astype(jnp.bfloat16)
    return (residual.astype(jnp.bfloat16), next_rows, next_scale)
```

```python
import functools

import jax
import jax.numpy as jnp
from jax import lax
from jax.experimental import pallas as pl
from jax.experimental.pallas import tpu as pltpu
from jax.sharding import PartitionSpec as P

MESH = pl.DeviceIdType.MESH
N_X = 4
N_Z = 2
WIDTH = 512
EARLY = 3
LAG = 2
LANES = 128


def exchange(
    tokens, gate, up, weight, gain,
    rows, square, peak,
    gate_v, up_v, weight_v, tokens_v, hidden, product, parts, partial, other,
    load, rs_send, rs_recv, z_send, z_recv, ag_send, ag_recv,
):
    n = product.shape[0]
    block = parts.shape[2]
    own = tokens_v.shape[0]
    me = lax.axis_index("tensor")
    x, z = me // N_Z, me % N_Z

    def along_x(d):
        return {"tensor": ((x + d) % N_X) * N_Z + z}

    along_z = {"tensor": x * N_Z + (1 - z)}

    barrier = pltpu.get_barrier_semaphore()
    for d in range(1, N_X):
        pl.semaphore_signal(barrier, inc=1, device_id=along_x(d), device_id_type=MESH)
    pl.semaphore_signal(barrier, inc=1, device_id=along_z, device_id_type=MESH)

    def weight_copy(c):
        columns = pl.ds(pl.multiple_of(c * WIDTH, WIDTH), WIDTH)
        return pltpu.make_async_copy(weight.at[:, columns], weight_v.at[c], load.at[3 + c])

    gate_copy = pltpu.make_async_copy(gate, gate_v, load.at[0])
    up_copy = pltpu.make_async_copy(up, up_v, load.at[1])
    tokens_copy = pltpu.make_async_copy(tokens, tokens_v, load.at[2])
    gate_copy.start()
    up_copy.start()
    for c in range(n):
        weight_copy(c).start()
    tokens_copy.start()

    gate_copy.wait()
    up_copy.wait()
    g = gate_v[...].astype(jnp.float32)
    hidden[...] = (g / (1.0 + jnp.exp(-g)) * up_v[...].astype(jnp.float32)).astype(hidden.dtype)

    def multiply(c):
        weight_copy(c).wait()
        product[c] = jnp.dot(
            hidden[...], weight_v[c], preferred_element_type=jnp.float32
        ).astype(product.dtype)

    def block_rows(i):
        return pl.ds(pl.multiple_of(i * block, block), block)

    def rs_copy(c, d):
        return pltpu.make_async_remote_copy(
            src_ref=product.at[c, block_rows((x + d) % N_X)],
            dst_ref=parts.at[c, d - 1],
            send_sem=rs_send.at[c, d - 1],
            recv_sem=rs_recv.at[c, d - 1],
            device_id=along_x(d),
            device_id_type=MESH,
        )

    def z_copy(c):
        return pltpu.make_async_remote_copy(
            src_ref=partial.at[c],
            dst_ref=other.at[c],
            send_sem=z_send.at[c],
            recv_sem=z_recv.at[c],
            device_id=along_z,
            device_id_type=MESH,
        )

    def ag_copy(c, d):
        return pltpu.make_async_remote_copy(
            src_ref=rows.at[c, block_rows(x)],
            dst_ref=rows.at[c, block_rows(x)],
            send_sem=ag_send.at[c, d - 1],
            recv_sem=ag_recv.at[c, d - 1],
            device_id=along_x(d),
            device_id_type=MESH,
        )

    def ag_arrival(c, d):
        return pltpu.make_async_remote_copy(
            src_ref=rows.at[c, block_rows((x + N_X - d) % N_X)],
            dst_ref=rows.at[c, block_rows((x + N_X - d) % N_X)],
            send_sem=ag_send.at[c, d - 1],
            recv_sem=ag_recv.at[c, d - 1],
            device_id=along_x(d),
            device_id_type=MESH,
        )

    def scatter(c):
        for d in (2, 1, 3):
            rs_copy(c, d).start()

    @pl.loop(0, EARLY)
    def _(c):
        multiply(c)

    pl.semaphore_wait(barrier, N_X)

    @pl.loop(0, EARLY)
    def _(c):
        scatter(c)

    @pl.loop(EARLY, n)
    def _(c):
        multiply(c)
        scatter(c)

    tokens_copy.wait()

    @pl.loop(0, n)
    def _(c):
        for d in range(1, N_X):
            rs_copy(c, d).wait_recv()
        total = product[c, block_rows(x)].astype(jnp.float32)
        for d in range(N_X - 1):
            total += parts[c, d].astype(jnp.float32)
        partial[c] = total.astype(partial.dtype)
        mine = pl.ds(pl.multiple_of(z * own, own), own)
        first = product[c, pl.ds(pl.multiple_of(x * block + z * own, own), own)].astype(jnp.float32)
        for d in range(N_X - 1):
            first += parts[c, d, mine].astype(jnp.float32)
        columns = pl.ds(pl.multiple_of(c * WIDTH, WIDTH), WIDTH)
        first += tokens_v[:, columns].astype(jnp.float32)
        partial[c, mine] = first.astype(partial.dtype)
        z_copy(c).start()

    square[...] = jnp.zeros_like(square)
    peak[...] = jnp.zeros_like(peak)

    def statistics(c):
        for d in range(1, N_X):
            ag_arrival(c, d).wait_recv()
        s, p = square[...], peak[...]
        for k in range(WIDTH // LANES):
            r = rows[c, :, k * LANES : (k + 1) * LANES].astype(jnp.float32)
            weight_of = gain[:, pl.ds(pl.multiple_of(c * WIDTH + k * LANES, LANES), LANES)]
            s += r * r
            p = jnp.maximum(p, jnp.abs(r * weight_of))
        square[...] = s
        peak[...] = p

    @pl.loop(0, n)
    def _(c):
        z_copy(c).wait_recv()
        rows[c, block_rows(x)] = (
            partial[c].astype(jnp.float32) + other[c].astype(jnp.float32)
        ).astype(rows.dtype)
        for d in (2, 1, 3):
            ag_copy(c, d).start()

        @pl.when(c >= LAG)
        def _():
            statistics(c - LAG)

    @pl.loop(n - LAG, n)
    def _(c):
        statistics(c)

    @pl.loop(0, n)
    def _(c):
        for d in range(1, N_X):
            rs_copy(c, d).wait_send()
            ag_copy(c, d).wait_send()
        z_copy(c).wait_send()


def scale(rows, square, peak, gain, residual_out, next_rows, next_scale, staged, sem):
    n, tokens, _ = rows.shape
    own = residual_out.shape[0]
    me = lax.axis_index("tensor")
    mine = pl.ds(pl.multiple_of(me * own, own), own)
    columns = [slice(c * WIDTH, (c + 1) * WIDTH) for c in range(n)]
    for c in range(n):
        residual_out[:, columns[c]] = rows[c, mine]
    blocks = 4
    size = tokens // blocks
    copies = []
    for b in range(blocks):
        these = slice(b * size, (b + 1) * size)
        inverse = 1.0 / jnp.max(peak[these], axis=1, keepdims=True)
        for c in range(n):
            r = rows[c, these].astype(jnp.float32)
            staged[these, columns[c]] = (r * gain[:, columns[c]] * inverse).astype(staged.dtype)
        copies.append(pltpu.make_async_copy(staged.at[these], next_rows.at[these], sem.at[b]))
        copies[-1].start()
    features = n * WIDTH
    mean = jnp.sum(square[...].T, axis=0, keepdims=True) * (1.0 / features)
    next_scale[...] = jnp.max(peak[...].T, axis=0, keepdims=True) * lax.rsqrt(mean + 1e-05)
    for copy in copies:
        copy.wait()


def body(tokens, gate, up, weight, gain):
    own, features = tokens.shape
    count, hidden_units = gate.shape
    n = features // WIDTH
    block = own * N_Z
    gain = gain.reshape(1, features)
    tokens, gate, up, weight = (pltpu.with_memory_space_constraint(a, pltpu.HBM) for a in (tokens, gate, up, weight))
    vmem, hbm = pl.BlockSpec(memory_space=pltpu.VMEM), pl.BlockSpec(memory_space=pltpu.HBM)
    bf16, f32 = jnp.bfloat16, jnp.float32
    dma = pltpu.SemaphoreType.DMA
    rows, square, peak = pl.pallas_call(
        exchange,
        out_shape=(
            jax.ShapeDtypeStruct((n, count, WIDTH), bf16),
            jax.ShapeDtypeStruct((count, LANES), f32),
            jax.ShapeDtypeStruct((count, LANES), f32),
        ),
        in_specs=[hbm, hbm, hbm, hbm, vmem],
        out_specs=(vmem, vmem, vmem),
        scratch_shapes=[
            pltpu.VMEM((count, hidden_units), bf16),
            pltpu.VMEM((count, hidden_units), bf16),
            pltpu.VMEM((n, hidden_units, WIDTH), bf16),
            pltpu.VMEM((own, features), bf16),
            pltpu.VMEM((count, hidden_units), bf16),
            pltpu.VMEM((n, count, WIDTH), bf16),
            pltpu.VMEM((n, N_X - 1, block, WIDTH), bf16),
            pltpu.VMEM((n, block, WIDTH), bf16),
            pltpu.VMEM((n, block, WIDTH), bf16),
            dma((3 + n,)),
            dma((n, N_X - 1)),
            dma((n, N_X - 1)),
            dma((n,)),
            dma((n,)),
            dma((n, N_X - 1)),
            dma((n, N_X - 1)),
        ],
        compiler_params=pltpu.CompilerParams(collective_id=0, has_side_effects=True, vmem_limit_bytes=52_000_000),
        name="exchange",
    )(tokens, gate, up, weight, gain)
    residual_out, next_rows, next_scale = pl.pallas_call(
        scale,
        out_shape=(
            jax.ShapeDtypeStruct((own, features), bf16),
            jax.ShapeDtypeStruct((count, features), bf16),
            jax.ShapeDtypeStruct((1, count), f32),
        ),
        in_specs=[vmem, vmem, vmem, vmem],
        out_specs=(vmem, hbm, vmem),
        scratch_shapes=[pltpu.VMEM((count, features), bf16), dma((4,))],
        compiler_params=pltpu.CompilerParams(vmem_limit_bytes=8 << 20),
        name="scale",
    )(rows, square, peak, gain)
    return residual_out, next_rows, next_scale.reshape(count)


def solution(mesh):
    return jax.shard_map(
        body,
        mesh=mesh,
        in_specs=(
            P(("dp", "tensor"), None),
            P("dp", "tensor"),
            P("dp", "tensor"),
            P("tensor", None),
            P(),
        ),
        out_specs=(P(("dp", "tensor"), None), P("dp", None), P("dp")),
        check_vma=False,
    )
```

```python
import contextlib

import jax
import jax.numpy as jnp
from jax import lax
from jax.experimental import pallas as pl
from jax.experimental.pallas import tpu as pltpu
from jax.sharding import PartitionSpec as P

MESH = pl.DeviceIdType.MESH
N_X = 4
N_Z = 2
N_LO = 6
N_CORES = 2
WIDTH = 256
SPAN = 2
LAG = 4
LANES = 128
BLOCKS = 8
PACE = 3
AHEAD = 8


def scope(name):
    return contextlib.nullcontext()


def exchange(
    tokens, gate, up, weight, gain_in,
    rows, square, peak, gain,
    acts, weight_v, tokens_v, hidden, product, parts, partial, other,
    load, ready, rs_send, rs_recv, z_send, z_recv, ag_send, ag_recv,
):
    n = product.shape[0]
    block = parts.shape[2]
    own = tokens_v.shape[0]
    me = lax.axis_index("tensor")
    x, z = me // N_Z, me % N_Z

    turn = (lax.axis_index("dp") // N_CORES) % N_LO // 2

    def along_x(d):
        return {"tensor": ((x + d) % N_X) * N_Z + z}

    along_z = {"tensor": x * N_Z + (1 - z)}

    barrier = pltpu.get_barrier_semaphore()
    for d in range(1, N_X):
        pl.semaphore_signal(barrier, inc=1, device_id=along_x(d), device_id_type=MESH)

    @pl.when(z == 0)
    def _():
        pl.semaphore_signal(barrier, inc=1, device_id=along_z, device_id_type=MESH)

    def weight_copy(b):
        columns = pl.ds(pl.multiple_of(b * SPAN * WIDTH, WIDTH), SPAN * WIDTH)
        return pltpu.make_async_copy(weight.at[:, columns], weight_v.at[b], load.at[3 + b])

    gate_copy = pltpu.make_async_copy(gate, acts.at[0], load.at[0])
    up_copy = pltpu.make_async_copy(up, acts.at[1], load.at[0])
    tokens_copy = pltpu.make_async_copy(tokens, tokens_v, load.at[1])
    gain_copy = pltpu.make_async_copy(gain_in, gain, load.at[2])
    gate_copy.start()
    up_copy.start()
    weight_copy(0).start()
    with scope("load_wait"):
        pltpu.make_async_copy(acts, acts, load.at[0]).wait()
    for b in range(1, n // SPAN):
        weight_copy(b).start()
    tokens_copy.start()
    gain_copy.start()
    g = acts[0].astype(jnp.float32)
    hidden[...] = (g / (1.0 + jnp.exp(-g)) * acts[1].astype(jnp.float32)).astype(hidden.dtype)

    def multiply(b):
        weight_copy(b).wait()
        result = jnp.dot(hidden[...], weight_v[b], preferred_element_type=jnp.float32)
        for k in range(SPAN):
            product[b * SPAN + k] = result[:, k * WIDTH : (k + 1) * WIDTH].astype(product.dtype)

    def block_rows(i):
        return pl.ds(pl.multiple_of(i * block, block), block)

    def rs_copy(c, d):
        return pltpu.make_async_remote_copy(
            src_ref=product.at[c, block_rows((x + d) % N_X)],
            dst_ref=parts.at[c, d - 1],
            send_sem=rs_send,
            recv_sem=rs_recv.at[c],
            device_id=along_x(d),
            device_id_type=MESH,
        )

    def z_copy(c):
        return pltpu.make_async_remote_copy(
            src_ref=partial.at[c],
            dst_ref=other.at[c],
            send_sem=z_send,
            recv_sem=z_recv.at[c],
            device_id=along_z,
            device_id_type=MESH,
        )

    def z_copies(first, end):
        @pl.loop(first, end)
        def _(c):
            z_copy(c).start()

    def ag_copy(c, d):
        return pltpu.make_async_remote_copy(
            src_ref=rows.at[c, block_rows(x)],
            dst_ref=rows.at[c, block_rows(x)],
            send_sem=ag_send,
            recv_sem=ag_recv.at[c],
            device_id=along_x(d),
            device_id_type=MESH,
        )

    def arrived(of_three, sem):
        pltpu.make_async_copy(of_three, of_three, sem).wait()

    def scatter(c):
        for d in (2, 1, 3):
            rs_copy(c, d).start()

    with scope("barrier_w"):
        pl.semaphore_wait(barrier, N_X - 1 + z)

    @pl.when(z == 1)
    def _():
        pl.semaphore_signal(ready, inc=1, device_id=along_z, device_id_type=MESH)

    @pl.loop(0, n // SPAN)
    def _(b):
        with scope("mm"):
            multiply(b)
        for k in range(SPAN):
            scatter(b * SPAN + k)

    tokens_copy.wait()
    gain_copy.wait()

    @pl.loop(0, n)
    def _(c):
        with scope("rs_wait"):
            arrived(parts.at[c], rs_recv.at[c])
        total = product[c, block_rows(x)].astype(jnp.float32)
        for d in range(N_X - 1):
            total += parts[c, d].astype(jnp.float32)
        partial[c] = total.astype(partial.dtype)
        mine = pl.ds(pl.multiple_of(z * own, own), own)
        first = product[c, pl.ds(pl.multiple_of(x * block + z * own, own), own)].astype(jnp.float32)
        for d in range(N_X - 1):
            first += parts[c, d, mine].astype(jnp.float32)
        columns = pl.ds(pl.multiple_of(c * WIDTH, WIDTH), WIDTH)
        first += tokens_v[:, columns].astype(jnp.float32)
        partial[c, mine] = first.astype(partial.dtype)

        sent = (c * (PACE - turn) + PACE - 1) // PACE
        due = jnp.where(c == n - 1, n, ((c + 1) * (PACE - turn) + PACE - 1) // PACE)

        @pl.when(z == 1)
        def _():
            z_copies(sent, due)

    ahead = AHEAD + turn // 2

    @pl.when(z == 0)
    def _():
        with scope("ready_w"):
            pl.semaphore_wait(ready, 1)
        z_copies(0, ahead)

    square[...] = jnp.zeros_like(square)
    peak[...] = jnp.zeros_like(peak)

    def statistics(c):
        with scope("ag_wait"):
            arrived(parts.at[c], ag_recv.at[c])
        s, p = square[...], peak[...]
        for k in range(WIDTH // LANES):
            r = rows[c, :, k * LANES : (k + 1) * LANES].astype(jnp.float32)
            weight_of = gain[:, pl.ds(pl.multiple_of(c * WIDTH + k * LANES, LANES), LANES)]
            s += r * r
            p = jnp.maximum(p, jnp.abs(r * weight_of))
        square[...] = s
        peak[...] = p

    @pl.loop(0, n)
    def _(c):
        with scope("z_wait"):
            z_copy(c).wait_recv()
        rows[c, block_rows(x)] = (
            partial[c].astype(jnp.float32) + other[c].astype(jnp.float32)
        ).astype(rows.dtype)
        for d in (2, 1, 3):
            ag_copy(c, d).start()

        @pl.when((z == 0) & (c > 0) & (c + ahead <= n))
        def _():
            z_copy(c + ahead - 1).start()

        @pl.when(c >= LAG)
        def _():
            statistics(c - LAG)

    @pl.loop(n - LAG, n)
    def _(c):
        statistics(c)

    with scope("send_wait"):
        arrived(parts, rs_send)
        arrived(parts, ag_send)
        arrived(partial, z_send)


def scale(rows, square, peak, gain, residual_out, next_rows, next_scale, kept, staged, scales, sem):
    n, tokens, _ = rows.shape
    own = kept.shape[0]
    me = lax.axis_index("tensor")
    mine = pl.ds(pl.multiple_of(me * own, own), own)
    columns = [slice(c * WIDTH, (c + 1) * WIDTH) for c in range(n)]
    for c in range(n):
        kept[:, columns[c]] = rows[c, mine]
    size = tokens // BLOCKS
    copies = [pltpu.make_async_copy(kept, residual_out, sem.at[BLOCKS])]
    copies[-1].start()
    mean = jnp.sum(square[...].T, axis=0, keepdims=True) * (1.0 / (n * WIDTH))
    scales[...] = jnp.max(peak[...].T, axis=0, keepdims=True) * lax.rsqrt(mean + 1e-05)
    copies.append(pltpu.make_async_copy(scales, next_scale, sem.at[BLOCKS + 1]))
    copies[-1].start()
    for b in range(BLOCKS):
        these = slice(b * size, (b + 1) * size)
        inverse = 1.0 / jnp.max(peak[these], axis=1, keepdims=True)
        for c in range(n):
            r = rows[c, these].astype(jnp.float32)
            staged[these, columns[c]] = (r * gain[:, columns[c]] * inverse).astype(staged.dtype)
        copies.append(pltpu.make_async_copy(staged.at[these], next_rows.at[these], sem.at[b]))
        copies[-1].start()
    for copy in copies:
        copy.wait()


def body(tokens, gate, up, weight, gain):
    own, features = tokens.shape
    count, hidden_units = gate.shape
    n = features // WIDTH
    block = own * N_Z
    gain = gain.reshape(1, features)
    tokens, gate, up, weight, gain = (pltpu.with_memory_space_constraint(a, pltpu.HBM) for a in (tokens, gate, up, weight, gain))
    vmem, hbm = pl.BlockSpec(memory_space=pltpu.VMEM), pl.BlockSpec(memory_space=pltpu.HBM)
    bf16, f32 = jnp.bfloat16, jnp.float32
    dma = pltpu.SemaphoreType.DMA
    rows, square, peak, gain = pl.pallas_call(
        exchange,
        out_shape=(
            jax.ShapeDtypeStruct((n, count, WIDTH), bf16),
            jax.ShapeDtypeStruct((count, LANES), f32),
            jax.ShapeDtypeStruct((count, LANES), f32),
            jax.ShapeDtypeStruct((1, features), f32),
        ),
        in_specs=[hbm] * 5,
        out_specs=(vmem,) * 4,
        scratch_shapes=[
            pltpu.VMEM((2, count, hidden_units), bf16),
            pltpu.VMEM((n // SPAN, hidden_units, SPAN * WIDTH), bf16),
            pltpu.VMEM((own, features), bf16),
            pltpu.VMEM((count, hidden_units), bf16),
            pltpu.VMEM((n, count, WIDTH), bf16),
            pltpu.VMEM((n, N_X - 1, block, WIDTH), bf16),
            pltpu.VMEM((n, block, WIDTH), bf16),
            pltpu.VMEM((n, block, WIDTH), bf16),
            dma((3 + n // SPAN,)),
            pltpu.SemaphoreType.REGULAR,
            dma,
            dma((n,)),
            dma,
            dma((n,)),
            dma,
            dma((n,)),
        ],
        compiler_params=pltpu.CompilerParams(collective_id=0, has_side_effects=True, vmem_limit_bytes=52_000_000),
        name="exchange",
    )(tokens, gate, up, weight, gain)
    residual_out, next_rows, next_scale = pl.pallas_call(
        scale,
        out_shape=(
            jax.ShapeDtypeStruct((own, features), bf16),
            jax.ShapeDtypeStruct((count, features), bf16),
            jax.ShapeDtypeStruct((1, count), f32),
        ),
        in_specs=[vmem] * 4,
        out_specs=(hbm,) * 3,
        scratch_shapes=[
            pltpu.VMEM((own, features), bf16),
            pltpu.VMEM((count, features), bf16),
            pltpu.VMEM((1, count), f32),
            dma((BLOCKS + 2,)),
        ],
        compiler_params=pltpu.CompilerParams(vmem_limit_bytes=8 << 20),
        name="scale",
    )(rows, square, peak, gain)
    return residual_out, next_rows, next_scale.reshape(count)


def solution(mesh):
    return jax.shard_map(
        body,
        mesh=mesh,
        in_specs=(
            P(("dp", "tensor"), None),
            P("dp", "tensor"),
            P("dp", "tensor"),
            P("tensor", None),
            P(),
        ),
        out_specs=(P(("dp", "tensor"), None), P("dp", None), P("dp")),
        check_vma=False,
    )
```

```python
import contextlib

import jax
import jax.numpy as jnp
from jax import lax
from jax.experimental import pallas as pl
from jax.experimental.pallas import tpu as pltpu
from jax.sharding import PartitionSpec as P

MESH = pl.DeviceIdType.MESH
N_X = 4
N_Z = 2
N_LO = 6
N_CORES = 2
WIDTH = 256
SPAN = 2
LAG = 12
LANES = 128
BLOCKS = 8
PACE = 6
AHEAD = 4


def scope(name):
    return contextlib.nullcontext()


def exchange(
    tokens, gate, up, weight, gain_in,
    rows, square, peak, gain,
    acts, weight_v, tokens_v, hidden, product, parts, partial, other,
    load, ready, rs_send, rs_recv, z_send, z_recv, ag_send, ag_recv,
):
    n = product.shape[0]
    block = parts.shape[2]
    own = tokens_v.shape[0]
    me = lax.axis_index("tensor")
    x, z = me // N_Z, me % N_Z

    core, low = lax.axis_index("dp") % N_CORES, (lax.axis_index("dp") // N_CORES) % N_LO
    turn, odd = low // 2, low % 2
    pace = jnp.where(turn == 0, PACE, jnp.where(turn == 1, 4 + odd, PACE - 3 * odd))

    def along_x(d):
        return {"tensor": ((x + d) % N_X) * N_Z + z}

    along_z = {"tensor": x * N_Z + (1 - z)}

    barrier = pltpu.get_barrier_semaphore()
    for d in range(1, N_X):
        pl.semaphore_signal(barrier, inc=1, device_id=along_x(d), device_id_type=MESH)

    @pl.when(z == 0)
    def _():
        pl.semaphore_signal(barrier, inc=1, device_id=along_z, device_id_type=MESH)

    def weight_copy(b):
        columns = pl.ds(pl.multiple_of(b * SPAN * WIDTH, WIDTH), SPAN * WIDTH)
        return pltpu.make_async_copy(weight.at[:, columns], weight_v.at[b], load.at[3 + b])

    gate_copy = pltpu.make_async_copy(gate, acts.at[0], load.at[0])
    up_copy = pltpu.make_async_copy(up, acts.at[1], load.at[0])
    tokens_copy = pltpu.make_async_copy(tokens, tokens_v, load.at[1])
    gain_copy = pltpu.make_async_copy(gain_in, gain, load.at[2])
    gate_copy.start()
    up_copy.start()
    weight_copy(0).start()
    for b in range(1, n // SPAN):
        weight_copy(b).start()
    tokens_copy.start()
    gain_copy.start()
    with scope("load_wait"):
        pltpu.make_async_copy(acts, acts, load.at[0]).wait()
    g = acts[0].astype(jnp.float32)
    hidden[...] = (g / (1.0 + jnp.exp(-g)) * acts[1].astype(jnp.float32)).astype(hidden.dtype)

    def multiply(b):
        weight_copy(b).wait()
        result = jnp.dot(hidden[...], weight_v[b], preferred_element_type=jnp.float32)
        for k in range(SPAN):
            product[b * SPAN + k] = result[:, k * WIDTH : (k + 1) * WIDTH].astype(product.dtype)

    def block_rows(i):
        return pl.ds(pl.multiple_of(i * block, block), block)

    def rs_copy(c, d):
        return pltpu.make_async_remote_copy(
            src_ref=product.at[c, block_rows((x + d) % N_X)],
            dst_ref=parts.at[c, d - 1],
            send_sem=rs_send,
            recv_sem=rs_recv.at[c],
            device_id=along_x(d),
            device_id_type=MESH,
        )

    def z_copy(c):
        return pltpu.make_async_remote_copy(
            src_ref=partial.at[c],
            dst_ref=other.at[c],
            send_sem=z_send,
            recv_sem=z_recv.at[c],
            device_id=along_z,
            device_id_type=MESH,
        )

    def z_copies(first, end):
        @pl.loop(first, end)
        def _(c):
            z_copy(c).start()

    def ag_copy(c, d):
        return pltpu.make_async_remote_copy(
            src_ref=rows.at[c, block_rows(x)],
            dst_ref=rows.at[c, block_rows(x)],
            send_sem=ag_send,
            recv_sem=ag_recv.at[c],
            device_id=along_x(d),
            device_id_type=MESH,
        )

    def arrived(of_three, sem):
        pltpu.make_async_copy(of_three, of_three, sem).wait()

    def scatter(c):
        for d in (2, 1, 3):
            rs_copy(c, d).start()

    with scope("mm"):
        multiply(0)
    with scope("barrier_w"):
        pl.semaphore_wait(barrier, N_X - 1 + z)

    @pl.when(z == 1)
    def _():
        pl.semaphore_signal(ready, inc=1, device_id=along_z, device_id_type=MESH)

    for k in range(SPAN):
        scatter(k)

    @pl.loop(1, n // SPAN)
    def _(b):
        with scope("mm"):
            multiply(b)
        for k in range(SPAN):
            scatter(b * SPAN + k)

    tokens_copy.wait()
    gain_copy.wait()

    @pl.loop(0, n)
    def _(c):
        with scope("rs_wait"):
            arrived(parts.at[c], rs_recv.at[c])
        total = product[c, block_rows(x)].astype(jnp.float32)
        for d in range(N_X - 1):
            total += parts[c, d].astype(jnp.float32)
        partial[c] = total.astype(partial.dtype)
        mine = pl.ds(pl.multiple_of(z * own, own), own)
        first = product[c, pl.ds(pl.multiple_of(x * block + z * own, own), own)].astype(jnp.float32)
        for d in range(N_X - 1):
            first += parts[c, d, mine].astype(jnp.float32)
        columns = pl.ds(pl.multiple_of(c * WIDTH, WIDTH), WIDTH)
        first += tokens_v[:, columns].astype(jnp.float32)
        partial[c, mine] = first.astype(partial.dtype)

        sent = (c * pace + PACE - 1) // PACE
        due = jnp.where(c == n - 1, n, ((c + 1) * pace + PACE - 1) // PACE)

        @pl.when(z == 1)
        def _():
            z_copies(sent, due)

    ahead = AHEAD + 1 - 2 * core

    @pl.when(z == 0)
    def _():
        with scope("ready_w"):
            pl.semaphore_wait(ready, 1)
        z_copies(0, ahead)

    square[...] = jnp.zeros_like(square)
    peak[...] = jnp.zeros_like(peak)

    def statistics(c):
        with scope("ag_wait"):
            arrived(parts.at[c], ag_recv.at[c])
        s, p = square[...], peak[...]
        for k in range(WIDTH // LANES):
            r = rows[c, :, k * LANES : (k + 1) * LANES].astype(jnp.float32)
            weight_of = gain[:, pl.ds(pl.multiple_of(c * WIDTH + k * LANES, LANES), LANES)]
            s += r * r
            p = jnp.maximum(p, jnp.abs(r * weight_of))
        square[...] = s
        peak[...] = p

    @pl.loop(0, n)
    def _(c):
        with scope("z_wait"):
            z_copy(c).wait_recv()
        rows[c, block_rows(x)] = (
            partial[c].astype(jnp.float32) + other[c].astype(jnp.float32)
        ).astype(rows.dtype)
        for d in (2, 1, 3):
            ag_copy(c, d).start()

        @pl.when((z == 0) & (c > 0) & (c + ahead <= n))
        def _():
            z_copy(c + ahead - 1).start()

        @pl.when(c >= LAG)
        def _():
            statistics(c - LAG)

    @pl.loop(n - LAG, n)
    def _(c):
        statistics(c)

    with scope("send_wait"):
        arrived(parts, rs_send)
        arrived(parts, ag_send)
        arrived(partial, z_send)


def scale(rows, square, peak, gain, residual_out, next_rows, next_scale, kept, staged, scales, sem):
    n, tokens, _ = rows.shape
    own = kept.shape[0]
    me = lax.axis_index("tensor")
    mine = pl.ds(pl.multiple_of(me * own, own), own)
    columns = [slice(c * WIDTH, (c + 1) * WIDTH) for c in range(n)]
    for c in range(n):
        kept[:, columns[c]] = rows[c, mine]
    size = tokens // BLOCKS
    copies = [pltpu.make_async_copy(kept, residual_out, sem.at[BLOCKS])]
    copies[-1].start()
    mean = jnp.sum(square[...].T, axis=0, keepdims=True) * (1.0 / (n * WIDTH))
    scales[...] = jnp.max(peak[...].T, axis=0, keepdims=True) * lax.rsqrt(mean + 1e-05)
    copies.append(pltpu.make_async_copy(scales, next_scale, sem.at[BLOCKS + 1]))
    copies[-1].start()
    for b in range(BLOCKS):
        these = slice(b * size, (b + 1) * size)
        inverse = 1.0 / jnp.max(peak[these], axis=1, keepdims=True)
        for c in range(n):
            r = rows[c, these].astype(jnp.float32)
            staged[these, columns[c]] = (r * gain[:, columns[c]] * inverse).astype(staged.dtype)
        copies.append(pltpu.make_async_copy(staged.at[these], next_rows.at[these], sem.at[b]))
        copies[-1].start()
    for copy in copies:
        copy.wait()


def body(tokens, gate, up, weight, gain):
    own, features = tokens.shape
    count, hidden_units = gate.shape
    n = features // WIDTH
    block = own * N_Z
    gain = gain.reshape(1, features)
    tokens, gate, up, weight, gain = (pltpu.with_memory_space_constraint(a, pltpu.HBM) for a in (tokens, gate, up, weight, gain))
    vmem, hbm = pl.BlockSpec(memory_space=pltpu.VMEM), pl.BlockSpec(memory_space=pltpu.HBM)
    bf16, f32 = jnp.bfloat16, jnp.float32
    dma = pltpu.SemaphoreType.DMA
    rows, square, peak, gain = pl.pallas_call(
        exchange,
        out_shape=(
            jax.ShapeDtypeStruct((n, count, WIDTH), bf16),
            jax.ShapeDtypeStruct((count, LANES), f32),
            jax.ShapeDtypeStruct((count, LANES), f32),
            jax.ShapeDtypeStruct((1, features), f32),
        ),
        in_specs=[hbm] * 5,
        out_specs=(vmem,) * 4,
        scratch_shapes=[
            pltpu.VMEM((2, count, hidden_units), bf16),
            pltpu.VMEM((n // SPAN, hidden_units, SPAN * WIDTH), bf16),
            pltpu.VMEM((own, features), bf16),
            pltpu.VMEM((count, hidden_units), bf16),
            pltpu.VMEM((n, count, WIDTH), bf16),
            pltpu.VMEM((n, N_X - 1, block, WIDTH), bf16),
            pltpu.VMEM((n, block, WIDTH), bf16),
            pltpu.VMEM((n, block, WIDTH), bf16),
            dma((3 + n // SPAN,)),
            pltpu.SemaphoreType.REGULAR,
            dma,
            dma((n,)),
            dma,
            dma((n,)),
            dma,
            dma((n,)),
        ],
        compiler_params=pltpu.CompilerParams(collective_id=0, has_side_effects=True, vmem_limit_bytes=52_000_000),
        name="exchange",
    )(tokens, gate, up, weight, gain)
    residual_out, next_rows, next_scale = pl.pallas_call(
        scale,
        out_shape=(
            jax.ShapeDtypeStruct((own, features), bf16),
            jax.ShapeDtypeStruct((count, features), bf16),
            jax.ShapeDtypeStruct((1, count), f32),
        ),
        in_specs=[vmem] * 4,
        out_specs=(hbm,) * 3,
        scratch_shapes=[
            pltpu.VMEM((own, features), bf16),
            pltpu.VMEM((count, features), bf16),
            pltpu.VMEM((1, count), f32),
            dma((BLOCKS + 2,)),
        ],
        compiler_params=pltpu.CompilerParams(vmem_limit_bytes=8 << 20),
        name="scale",
    )(rows, square, peak, gain)
    return residual_out, next_rows, next_scale.reshape(count)


def solution(mesh):
    return jax.shard_map(
        body,
        mesh=mesh,
        in_specs=(
            P(("dp", "tensor"), None),
            P("dp", "tensor"),
            P("dp", "tensor"),
            P("tensor", None),
            P(),
        ),
        out_specs=(P(("dp", "tensor"), None), P("dp", None), P("dp")),
        check_vma=False,
    )
```

```python
import contextlib

import jax
import jax.numpy as jnp
from jax import lax
from jax.experimental import pallas as pl
from jax.experimental.pallas import tpu as pltpu
from jax.sharding import PartitionSpec as P

MESH = pl.DeviceIdType.MESH
N_X = 4
N_Z = 2
N_LO = 6
N_CORES = 2
WIDTH = 256
SPAN = 2
LAG = 12
LANES = 128
BLOCKS = 16
PACE = 6
AHEAD = 4


def scope(name):
    return contextlib.nullcontext()


def exchange(
    tokens, gate, up, weight, gain_in,
    rows, square, peak, gain,
    acts, weight_v, tokens_v, hidden, product, parts, partial, other,
    load, ready, rs_send, rs_recv, z_send, z_recv, ag_send, ag_recv,
):
    n = product.shape[0]
    block = parts.shape[2]
    own = tokens_v.shape[0]
    me = lax.axis_index("tensor")
    x, z = me // N_Z, me % N_Z

    core, low = lax.axis_index("dp") % N_CORES, (lax.axis_index("dp") // N_CORES) % N_LO
    turn, odd = low // 2, low % 2
    pace = jnp.where(turn == 0, PACE, jnp.where(turn == 1, 4 + odd, PACE - 3 * odd))

    def along_x(d):
        return {"tensor": ((x + d) % N_X) * N_Z + z}

    along_z = {"tensor": x * N_Z + (1 - z)}

    barrier = pltpu.get_barrier_semaphore()
    for d in range(1, N_X):
        pl.semaphore_signal(barrier, inc=1, device_id=along_x(d), device_id_type=MESH)

    @pl.when(z == 0)
    def _():
        pl.semaphore_signal(barrier, inc=1, device_id=along_z, device_id_type=MESH)

    def weight_copy(b):
        columns = pl.ds(pl.multiple_of(b * SPAN * WIDTH, WIDTH), SPAN * WIDTH)
        return pltpu.make_async_copy(weight.at[:, columns], weight_v.at[b], load.at[3 + b])

    def first_copy(k):
        columns = pl.ds(k * WIDTH, WIDTH)
        place = load.at[3 if k == 0 else 2 + n // SPAN + k]
        return pltpu.make_async_copy(weight.at[:, columns], weight_v.at[0, :, columns], place)

    gate_copy = pltpu.make_async_copy(gate, acts.at[0], load.at[0])
    up_copy = pltpu.make_async_copy(up, acts.at[1], load.at[0])
    tokens_copy = pltpu.make_async_copy(tokens, tokens_v, load.at[1])
    gain_copy = pltpu.make_async_copy(gain_in, gain, load.at[2])
    gate_copy.start()
    up_copy.start()
    for k in range(SPAN):
        first_copy(k).start()
    for b in range(1, n // SPAN):
        weight_copy(b).start()
    tokens_copy.start()
    gain_copy.start()
    with scope("load_wait"):
        pltpu.make_async_copy(acts, acts, load.at[0]).wait()
    g = acts[0].astype(jnp.float32)
    hidden[...] = (g / (1.0 + jnp.exp(-g)) * acts[1].astype(jnp.float32)).astype(hidden.dtype)

    def multiply_first(k):
        first_copy(k).wait()
        product[k] = jnp.dot(
            hidden[...], weight_v[0, :, k * WIDTH : (k + 1) * WIDTH], preferred_element_type=jnp.float32
        ).astype(product.dtype)

    def multiply(b):
        weight_copy(b).wait()
        result = jnp.dot(hidden[...], weight_v[b], preferred_element_type=jnp.float32)
        for k in range(SPAN):
            product[b * SPAN + k] = result[:, k * WIDTH : (k + 1) * WIDTH].astype(product.dtype)

    def block_rows(i):
        return pl.ds(pl.multiple_of(i * block, block), block)

    def rs_copy(c, d):
        return pltpu.make_async_remote_copy(
            src_ref=product.at[c, block_rows((x + d) % N_X)],
            dst_ref=parts.at[c, d - 1],
            send_sem=rs_send,
            recv_sem=rs_recv.at[c],
            device_id=along_x(d),
            device_id_type=MESH,
        )

    def z_copy(c):
        return pltpu.make_async_remote_copy(
            src_ref=partial.at[c],
            dst_ref=other.at[c],
            send_sem=z_send,
            recv_sem=z_recv.at[c],
            device_id=along_z,
            device_id_type=MESH,
        )

    def z_copies(first, end):
        @pl.loop(first, end)
        def _(c):
            z_copy(c).start()

    def ag_copy(c, d):
        return pltpu.make_async_remote_copy(
            src_ref=rows.at[c, block_rows(x)],
            dst_ref=rows.at[c, block_rows(x)],
            send_sem=ag_send,
            recv_sem=ag_recv.at[c],
            device_id=along_x(d),
            device_id_type=MESH,
        )

    def arrived(of_three, sem):
        pltpu.make_async_copy(of_three, of_three, sem).wait()

    def scatter(c):
        for d in (2, 1, 3):
            rs_copy(c, d).start()

    with scope("mm"):
        multiply_first(0)
    with scope("barrier_w"):
        pl.semaphore_wait(barrier, N_X - 1 + z)

    @pl.when(z == 1)
    def _():
        pl.semaphore_signal(ready, inc=1, device_id=along_z, device_id_type=MESH)

    scatter(0)
    for k in range(1, SPAN):
        multiply_first(k)
        scatter(k)

    @pl.loop(1, n // SPAN)
    def _(b):
        with scope("mm"):
            multiply(b)
        for k in range(SPAN):
            scatter(b * SPAN + k)

    tokens_copy.wait()
    gain_copy.wait()

    @pl.loop(0, n)
    def _(c):
        with scope("rs_wait"):
            arrived(parts.at[c], rs_recv.at[c])
        total = product[c, block_rows(x)].astype(jnp.float32)
        for d in range(N_X - 1):
            total += parts[c, d].astype(jnp.float32)
        partial[c] = total.astype(partial.dtype)
        mine = pl.ds(pl.multiple_of(z * own, own), own)
        first = product[c, pl.ds(pl.multiple_of(x * block + z * own, own), own)].astype(jnp.float32)
        for d in range(N_X - 1):
            first += parts[c, d, mine].astype(jnp.float32)
        columns = pl.ds(pl.multiple_of(c * WIDTH, WIDTH), WIDTH)
        first += tokens_v[:, columns].astype(jnp.float32)
        partial[c, mine] = first.astype(partial.dtype)

        sent = (c * pace + PACE - 1) // PACE
        due = jnp.where(c == n - 1, n, ((c + 1) * pace + PACE - 1) // PACE)

        @pl.when(z == 1)
        def _():
            z_copies(sent, due)

    ahead = AHEAD + 1 - 2 * core

    @pl.when(z == 0)
    def _():
        with scope("ready_w"):
            pl.semaphore_wait(ready, 1)
        z_copies(0, ahead)

    square[...] = jnp.zeros_like(square)
    peak[...] = jnp.zeros_like(peak)

    def statistics(c):
        with scope("ag_wait"):
            arrived(parts.at[c], ag_recv.at[c])
        s, p = square[...], peak[...]
        for k in range(WIDTH // LANES):
            r = rows[c, :, k * LANES : (k + 1) * LANES].astype(jnp.float32)
            weight_of = gain[:, pl.ds(pl.multiple_of(c * WIDTH + k * LANES, LANES), LANES)]
            s += r * r
            p = jnp.maximum(p, jnp.abs(r * weight_of))
        square[...] = s
        peak[...] = p

    @pl.loop(0, n)
    def _(c):
        with scope("z_wait"):
            z_copy(c).wait_recv()
        rows[c, block_rows(x)] = (
            partial[c].astype(jnp.float32) + other[c].astype(jnp.float32)
        ).astype(rows.dtype)
        for d in (2, 1, 3):
            ag_copy(c, d).start()

        @pl.when((z == 0) & (c > 0) & (c + ahead <= n))
        def _():
            z_copy(c + ahead - 1).start()

        @pl.when(c >= LAG)
        def _():
            statistics(c - LAG)

    @pl.loop(n - LAG, n)
    def _(c):
        statistics(c)

    with scope("send_wait"):
        arrived(parts, rs_send)
        arrived(parts, ag_send)
        arrived(partial, z_send)


def scale(rows, square, peak, gain, residual_out, next_rows, next_scale, kept, staged, scales, sem):
    n, tokens, _ = rows.shape
    own = kept.shape[0]
    me = lax.axis_index("tensor")
    mine = pl.ds(pl.multiple_of(me * own, own), own)
    columns = [slice(c * WIDTH, (c + 1) * WIDTH) for c in range(n)]
    for c in range(n):
        kept[:, columns[c]] = rows[c, mine]
    size = tokens // BLOCKS
    copies = [pltpu.make_async_copy(kept, residual_out, sem.at[BLOCKS])]
    copies[-1].start()
    mean = jnp.sum(square[...].T, axis=0, keepdims=True) * (1.0 / (n * WIDTH))
    scales[...] = jnp.max(peak[...].T, axis=0, keepdims=True) * lax.rsqrt(mean + 1e-05)
    copies.append(pltpu.make_async_copy(scales, next_scale, sem.at[BLOCKS + 1]))
    copies[-1].start()
    for b in range(BLOCKS):
        these = slice(b * size, (b + 1) * size)
        inverse = 1.0 / jnp.max(peak[these], axis=1, keepdims=True)
        for c in range(n):
            r = rows[c, these].astype(jnp.float32)
            staged[these, columns[c]] = (r * gain[:, columns[c]] * inverse).astype(staged.dtype)
        copies.append(pltpu.make_async_copy(staged.at[these], next_rows.at[these], sem.at[b]))
        copies[-1].start()
    for copy in copies:
        copy.wait()


def body(tokens, gate, up, weight, gain):
    own, features = tokens.shape
    count, hidden_units = gate.shape
    n = features // WIDTH
    block = own * N_Z
    gain = gain.reshape(1, features)
    tokens, gate, up, weight, gain = (pltpu.with_memory_space_constraint(a, pltpu.HBM) for a in (tokens, gate, up, weight, gain))
    vmem, hbm = pl.BlockSpec(memory_space=pltpu.VMEM), pl.BlockSpec(memory_space=pltpu.HBM)
    bf16, f32 = jnp.bfloat16, jnp.float32
    dma = pltpu.SemaphoreType.DMA
    rows, square, peak, gain = pl.pallas_call(
        exchange,
        out_shape=(
            jax.ShapeDtypeStruct((n, count, WIDTH), bf16),
            jax.ShapeDtypeStruct((count, LANES), f32),
            jax.ShapeDtypeStruct((count, LANES), f32),
            jax.ShapeDtypeStruct((1, features), f32),
        ),
        in_specs=[hbm] * 5,
        out_specs=(vmem,) * 4,
        scratch_shapes=[
            pltpu.VMEM((2, count, hidden_units), bf16),
            pltpu.VMEM((n // SPAN, hidden_units, SPAN * WIDTH), bf16),
            pltpu.VMEM((own, features), bf16),
            pltpu.VMEM((count, hidden_units), bf16),
            pltpu.VMEM((n, count, WIDTH), bf16),
            pltpu.VMEM((n, N_X - 1, block, WIDTH), bf16),
            pltpu.VMEM((n, block, WIDTH), bf16),
            pltpu.VMEM((n, block, WIDTH), bf16),
            dma((2 + n // SPAN + SPAN,)),
            pltpu.SemaphoreType.REGULAR,
            dma,
            dma((n,)),
            dma,
            dma((n,)),
            dma,
            dma((n,)),
        ],
        compiler_params=pltpu.CompilerParams(collective_id=0, has_side_effects=True, vmem_limit_bytes=52_000_000),
        name="exchange",
    )(tokens, gate, up, weight, gain)
    residual_out, next_rows, next_scale = pl.pallas_call(
        scale,
        out_shape=(
            jax.ShapeDtypeStruct((own, features), bf16),
            jax.ShapeDtypeStruct((count, features), bf16),
            jax.ShapeDtypeStruct((1, count), f32),
        ),
        in_specs=[vmem] * 4,
        out_specs=(hbm,) * 3,
        scratch_shapes=[
            pltpu.VMEM((own, features), bf16),
            pltpu.VMEM((count, features), bf16),
            pltpu.VMEM((1, count), f32),
            dma((BLOCKS + 2,)),
        ],
        compiler_params=pltpu.CompilerParams(vmem_limit_bytes=8 << 20),
        name="scale",
    )(rows, square, peak, gain)
    return residual_out, next_rows, next_scale.reshape(count)


def solution(mesh):
    return jax.shard_map(
        body,
        mesh=mesh,
        in_specs=(
            P(("dp", "tensor"), None),
            P("dp", "tensor"),
            P("dp", "tensor"),
            P("tensor", None),
            P(),
        ),
        out_specs=(P(("dp", "tensor"), None), P("dp", None), P("dp")),
        check_vma=False,
    )
```

```python
import contextlib

import jax
import jax.numpy as jnp
from jax import lax
from jax.experimental import pallas as pl
from jax.experimental.pallas import tpu as pltpu
from jax.sharding import PartitionSpec as P

MESH = pl.DeviceIdType.MESH
N_X = 4
N_Z = 2
N_LO = 6
N_CORES = 2
WIDTH = 256
SPAN = 2
LAG = 12
LANES = 128
BLOCKS = 16
PACE = 6
AHEAD = 4


def scope(name):
    return contextlib.nullcontext()


def exchange(
    tokens, gate, up, weight, gain_in,
    rows, square, peak, gain,
    acts, weight_v, tokens_v, hidden, product, parts, partial, other,
    load, ready, rs_send, rs_recv, z_send, z_recv, ag_send, ag_recv,
):
    n = product.shape[0]
    block = parts.shape[2]
    own = tokens_v.shape[0]
    me = lax.axis_index("tensor")
    x, z = me // N_Z, me % N_Z

    core, low = lax.axis_index("dp") % N_CORES, (lax.axis_index("dp") // N_CORES) % N_LO
    turn, odd = low // 2, low % 2
    pace = jnp.where(turn == 0, PACE, jnp.where(turn == 1, 4 + odd, PACE - 3 * odd))

    def along_x(d):
        return {"tensor": ((x + d) % N_X) * N_Z + z}

    along_z = {"tensor": x * N_Z + (1 - z)}

    barrier = pltpu.get_barrier_semaphore()
    for d in range(1, N_X):
        pl.semaphore_signal(barrier, inc=1, device_id=along_x(d), device_id_type=MESH)

    @pl.when(z == 0)
    def _():
        pl.semaphore_signal(barrier, inc=1, device_id=along_z, device_id_type=MESH)

    def weight_copy(b):
        columns = pl.ds(pl.multiple_of(b * SPAN * WIDTH, WIDTH), SPAN * WIDTH)
        return pltpu.make_async_copy(weight.at[:, columns], weight_v.at[b], load.at[3 + b])

    def first_copy(k):
        columns = pl.ds(k * WIDTH, WIDTH)
        place = load.at[3 if k == 0 else 2 + n // SPAN + k]
        return pltpu.make_async_copy(weight.at[:, columns], weight_v.at[0, :, columns], place)

    gate_copy = pltpu.make_async_copy(gate, acts.at[0], load.at[0])
    up_copy = pltpu.make_async_copy(up, acts.at[1], load.at[0])
    tokens_copy = pltpu.make_async_copy(tokens, tokens_v, load.at[1])
    gain_copy = pltpu.make_async_copy(gain_in, gain, load.at[2])
    gate_copy.start()
    up_copy.start()
    for k in range(SPAN):
        first_copy(k).start()
    for b in range(1, n // SPAN):
        weight_copy(b).start()
    tokens_copy.start()
    gain_copy.start()
    with scope("load_wait"):
        pltpu.make_async_copy(acts, acts, load.at[0]).wait()
    g = acts[0].astype(jnp.float32)
    hidden[...] = (g / (1.0 + jnp.exp(-g)) * acts[1].astype(jnp.float32)).astype(hidden.dtype)

    def multiply_first(k):
        first_copy(k).wait()
        product[k] = jnp.dot(
            hidden[...], weight_v[0, :, k * WIDTH : (k + 1) * WIDTH], preferred_element_type=jnp.float32
        ).astype(product.dtype)

    def multiply(b):
        weight_copy(b).wait()
        result = jnp.dot(hidden[...], weight_v[b], preferred_element_type=jnp.float32)
        for k in range(SPAN):
            product[b * SPAN + k] = result[:, k * WIDTH : (k + 1) * WIDTH].astype(product.dtype)

    def block_rows(i):
        return pl.ds(pl.multiple_of(i * block, block), block)

    def rs_copy(c, d):
        return pltpu.make_async_remote_copy(
            src_ref=product.at[c, block_rows((x + d) % N_X)],
            dst_ref=parts.at[c, d - 1],
            send_sem=rs_send,
            recv_sem=rs_recv.at[c],
            device_id=along_x(d),
            device_id_type=MESH,
        )

    def z_copy(c):
        return pltpu.make_async_remote_copy(
            src_ref=partial.at[c],
            dst_ref=other.at[c],
            send_sem=z_send,
            recv_sem=z_recv.at[c],
            device_id=along_z,
            device_id_type=MESH,
        )

    def z_copies(first, end):
        @pl.loop(first, end)
        def _(c):
            z_copy(c).start()

    def ag_copy(c, d):
        return pltpu.make_async_remote_copy(
            src_ref=rows.at[c, block_rows(x)],
            dst_ref=rows.at[c, block_rows(x)],
            send_sem=ag_send,
            recv_sem=ag_recv.at[jnp.maximum(c - LAG + 1, 0)],
            device_id=along_x(d),
            device_id_type=MESH,
        )

    def arrived(of_three, sem):
        pltpu.make_async_copy(of_three, of_three, sem).wait()

    def scatter(c):
        for d in (2, 1, 3):
            rs_copy(c, d).start()

    with scope("mm"):
        multiply_first(0)
    with scope("barrier_w"):
        pl.semaphore_wait(barrier, N_X - 1 + z)

    @pl.when(z == 1)
    def _():
        pl.semaphore_signal(ready, inc=1, device_id=along_z, device_id_type=MESH)

    scatter(0)
    for k in range(1, SPAN):
        multiply_first(k)
        scatter(k)

    @pl.loop(1, n // SPAN)
    def _(b):
        with scope("mm"):
            multiply(b)
        for k in range(SPAN):
            scatter(b * SPAN + k)

    tokens_copy.wait()
    gain_copy.wait()

    @pl.loop(0, n)
    def _(c):
        with scope("rs_wait"):
            arrived(parts.at[c], rs_recv.at[c])
        total = product[c, block_rows(x)].astype(jnp.float32)
        for d in range(N_X - 1):
            total += parts[c, d].astype(jnp.float32)
        partial[c] = total.astype(partial.dtype)
        mine = pl.ds(pl.multiple_of(z * own, own), own)
        first = product[c, pl.ds(pl.multiple_of(x * block + z * own, own), own)].astype(jnp.float32)
        for d in range(N_X - 1):
            first += parts[c, d, mine].astype(jnp.float32)
        columns = pl.ds(pl.multiple_of(c * WIDTH, WIDTH), WIDTH)
        first += tokens_v[:, columns].astype(jnp.float32)
        partial[c, mine] = first.astype(partial.dtype)

        sent = (c * pace + PACE - 1) // PACE
        due = jnp.where(c == n - 1, n, ((c + 1) * pace + PACE - 1) // PACE)

        @pl.when(z == 1)
        def _():
            z_copies(sent, due)

    ahead = AHEAD + 1 - 2 * core

    @pl.when(z == 0)
    def _():
        with scope("ready_w"):
            pl.semaphore_wait(ready, 1)
        z_copies(0, ahead)

    square[...] = jnp.zeros_like(square)
    peak[...] = jnp.zeros_like(peak)

    def statistics(c):
        s, p = square[...], peak[...]
        for k in range(WIDTH // LANES):
            r = rows[c, :, k * LANES : (k + 1) * LANES].astype(jnp.float32)
            weight_of = gain[:, pl.ds(pl.multiple_of(c * WIDTH + k * LANES, LANES), LANES)]
            s += r * r
            p = jnp.maximum(p, jnp.abs(r * weight_of))
        square[...] = s
        peak[...] = p

    @pl.loop(0, n)
    def _(c):
        with scope("z_wait"):
            z_copy(c).wait_recv()
        rows[c, block_rows(x)] = (
            partial[c].astype(jnp.float32) + other[c].astype(jnp.float32)
        ).astype(rows.dtype)
        for d in (2, 1, 3):
            ag_copy(c, d).start()

        @pl.when((z == 0) & (c > 0) & (c + ahead <= n))
        def _():
            z_copy(c + ahead - 1).start()

    with scope("ag_wait"):
        arrived(parts.at[pl.ds(0, LAG)], ag_recv.at[0])

    @pl.loop(0, LAG)
    def _(c):
        statistics(c)

    @pl.loop(LAG, n)
    def _(c):
        with scope("ag_wait"):
            arrived(parts.at[c], ag_recv.at[c - LAG + 1])
        statistics(c)

    with scope("send_wait"):
        arrived(parts, rs_send)
        arrived(parts, ag_send)
        arrived(partial, z_send)


def scale(rows, square, peak, gain, residual_out, next_rows, next_scale, kept, staged, scales, sem):
    n, tokens, _ = rows.shape
    own = kept.shape[0]
    me = lax.axis_index("tensor")
    mine = pl.ds(pl.multiple_of(me * own, own), own)
    columns = [slice(c * WIDTH, (c + 1) * WIDTH) for c in range(n)]
    for c in range(n):
        kept[:, columns[c]] = rows[c, mine]
    size = tokens // BLOCKS
    copies = [pltpu.make_async_copy(kept, residual_out, sem.at[BLOCKS])]
    copies[-1].start()
    mean = jnp.sum(square[...].T, axis=0, keepdims=True) * (1.0 / (n * WIDTH))
    scales[...] = jnp.max(peak[...].T, axis=0, keepdims=True) * lax.rsqrt(mean + 1e-05)
    copies.append(pltpu.make_async_copy(scales, next_scale, sem.at[BLOCKS + 1]))
    copies[-1].start()
    for b in range(BLOCKS):
        these = slice(b * size, (b + 1) * size)
        inverse = 1.0 / jnp.max(peak[these], axis=1, keepdims=True)
        for c in range(n):
            r = rows[c, these].astype(jnp.float32)
            staged[these, columns[c]] = (r * gain[:, columns[c]] * inverse).astype(staged.dtype)
        copies.append(pltpu.make_async_copy(staged.at[these], next_rows.at[these], sem.at[b]))
        copies[-1].start()
    for copy in copies:
        copy.wait()


def body(tokens, gate, up, weight, gain):
    own, features = tokens.shape
    count, hidden_units = gate.shape
    n = features // WIDTH
    block = own * N_Z
    gain = gain.reshape(1, features)
    tokens, gate, up, weight, gain = (pltpu.with_memory_space_constraint(a, pltpu.HBM) for a in (tokens, gate, up, weight, gain))
    vmem, hbm = pl.BlockSpec(memory_space=pltpu.VMEM), pl.BlockSpec(memory_space=pltpu.HBM)
    bf16, f32 = jnp.bfloat16, jnp.float32
    dma = pltpu.SemaphoreType.DMA
    rows, square, peak, gain = pl.pallas_call(
        exchange,
        out_shape=(
            jax.ShapeDtypeStruct((n, count, WIDTH), bf16),
            jax.ShapeDtypeStruct((count, LANES), f32),
            jax.ShapeDtypeStruct((count, LANES), f32),
            jax.ShapeDtypeStruct((1, features), f32),
        ),
        in_specs=[hbm] * 5,
        out_specs=(vmem,) * 4,
        scratch_shapes=[
            pltpu.VMEM((2, count, hidden_units), bf16),
            pltpu.VMEM((n // SPAN, hidden_units, SPAN * WIDTH), bf16),
            pltpu.VMEM((own, features), bf16),
            pltpu.VMEM((count, hidden_units), bf16),
            pltpu.VMEM((n, count, WIDTH), bf16),
            pltpu.VMEM((n, N_X - 1, block, WIDTH), bf16),
            pltpu.VMEM((n, block, WIDTH), bf16),
            pltpu.VMEM((n, block, WIDTH), bf16),
            dma((2 + n // SPAN + SPAN,)),
            pltpu.SemaphoreType.REGULAR,
            dma,
            dma((n,)),
            dma,
            dma((n,)),
            dma,
            dma((n - LAG + 1,)),
        ],
        compiler_params=pltpu.CompilerParams(collective_id=0, has_side_effects=True, vmem_limit_bytes=52_000_000),
        name="exchange",
    )(tokens, gate, up, weight, gain)
    residual_out, next_rows, next_scale = pl.pallas_call(
        scale,
        out_shape=(
            jax.ShapeDtypeStruct((own, features), bf16),
            jax.ShapeDtypeStruct((count, features), bf16),
            jax.ShapeDtypeStruct((1, count), f32),
        ),
        in_specs=[vmem] * 4,
        out_specs=(hbm,) * 3,
        scratch_shapes=[
            pltpu.VMEM((own, features), bf16),
            pltpu.VMEM((count, features), bf16),
            pltpu.VMEM((1, count), f32),
            dma((BLOCKS + 2,)),
        ],
        compiler_params=pltpu.CompilerParams(vmem_limit_bytes=8 << 20),
        name="scale",
    )(rows, square, peak, gain)
    return residual_out, next_rows, next_scale.reshape(count)


def solution(mesh):
    return jax.shard_map(
        body,
        mesh=mesh,
        in_specs=(
            P(("dp", "tensor"), None),
            P("dp", "tensor"),
            P("dp", "tensor"),
            P("tensor", None),
            P(),
        ),
        out_specs=(P(("dp", "tensor"), None), P("dp", None), P("dp")),
        check_vma=False,
    )
```
